32 devices in a mesh: box: 8 (over z, y), nbr: 4 (over x, core).
Axes of the slice: x: 2, y: 2, z: 4, core: 2. Of those that a mesh axis runs over, the one named last changes fastest.
Arguments:
- self_block: float32 [64, 256, 256], P('box', 'nbr'), as said below
- ordering: int32 [64, 256], P('box'), may hold values from 0 to 255, each once within a row
- interp: float32 [64, 64, 192], P('box'), may hold values from -0.12 to 0.12
- near_band: float32 [64, 8, 2, 64, 256], P('box', 'nbr'), may hold values from -3 to 3
- pair_mask: int32 [64, 8], P('box', 'nbr'), may hold values 0 or 1
Outputs:
- skeleton_self: float32 [64, 64, 64], P('box')
- red_inverse: float32 [64, 192, 192], P('box', 'nbr')
- couplings: float32 [64, 8, 64, 128], P('box', 'nbr')
The draws below stay inside these ranges and needn't reach their ends.
Inputs may be any that keep to these rules, and one draw needn't show every extreme that they name: Each row of ordering is a permutation of the 256 unknowns of its box. Each self_block[b] has a positive diagonal.
All inputs are finite; a program needn't handle non-finite values. No bound on the sum of `pair_mask` on one device may be relied on, other than what follows from the above.
Results may differ from the reference program's by a relative error of at most 0.0003.
Values sent between devices are 32-bit elements; how exact they have to be, the bound alone decides.
A program may use at most 128 MiB of HBM per device.

```python
import jax
import jax.numpy as jnp
from jax import lax

PTS = 256
SKEL = 64
RED = 192
REACH = 4
OFFS = 8
NS_ITERS = 3
BOX_DEV = 8
BOXES = 64


def draw_self_block(key, part):
    first_key, second_key = jax.random.split(jax.random.fold_in(key, 17), 2)
    diag_vals = jax.random.uniform(first_key, (BOXES, PTS), jnp.float32, 8.0, 16.0)
    spread = 0.2 * jnp.clip(jax.random.normal(second_key, (BOXES, PTS, PTS), jnp.float32), -4.0, 4.0)
    identity = jnp.eye(PTS, dtype=jnp.float32)[None]
    return spread * (1.0 - identity) + identity * diag_vals[:, None, :]


def set_ends(values, own_key, least, top_value):
    index_at = [jax.random.randint(jax.random.fold_in(own_key, axis), (), 0, length) for axis, length in enumerate(values.shape)]
    longest = values.shape.index(max(values.shape))
    beside = index_at[:longest] + [(index_at[longest] + 1) % values.shape[longest]] + index_at[longest + 1:]
    return values.at[tuple(index_at)].set(least).at[tuple(beside)].set(top_value)


def shard_levels(own_key, extent, cuts, smallest, largest):
    factor_of = 1.0
    for axis_at, shards_of in cuts:
        heights = jax.random.uniform(jax.random.fold_in(jax.random.fold_in(own_key, 6), axis_at), (shards_of,), jnp.float32, smallest / len(cuts), largest / len(cuts))
        factor_of = factor_of * jnp.repeat(jnp.exp(heights), extent[axis_at] // shards_of).reshape((-1,) + (1,) * (len(extent) - 1 - axis_at))
    return factor_of


def gaussian(stream_key, dims, scale, reach, cuts=(), kind=jnp.bfloat16):
    entries = jax.random.normal(stream_key, dims, jnp.float32) * scale
    if len(cuts) > 0:
        entries = shard_levels(stream_key, dims, cuts, -0.22, 0.18) * entries
    return jnp.clip(entries, min=-reach, max=reach).astype(kind)


def setup_inputs(seed: int = 0) -> dict:
    key_of = jax.random.split(jax.random.key(seed), 6)
    return {
        "self_block": draw_self_block(jax.random.fold_in(key_of[5], 71), 0),
        "ordering": jax.vmap(lambda own: jax.random.permutation(own, PTS))(jax.random.split(key_of[1], BOXES)).reshape((BOXES, PTS)).astype(jnp.int32),
        "interp": gaussian(key_of[2], (BOXES, SKEL, RED), 0.02, 0.12, ((0, 8),), jnp.float32),
        "near_band": gaussian(key_of[3], (BOXES, OFFS, 2, SKEL, PTS), 0.5, 3.0, ((0, 8), (1, 4)), jnp.float32),
        "pair_mask": set_ends((jax.random.randint(key_of[4], (BOXES, OFFS), 0, 4) < 3).astype(jnp.int32), jax.random.fold_in(key_of[4], 1), 0, 1),
    }


def product(pattern, left_term, right_term):
    return jnp.einsum(pattern, left_term, right_term, precision=lax.Precision.HIGHEST)


def permuted(matrix, ordering):
    row_sorted = jnp.take_along_axis(matrix, ordering[:, :, None], axis=1)
    return jnp.take_along_axis(row_sorted, ordering[:, None, :], axis=2)


def factors(matrix, ordering, interp):
    full_block = permuted(matrix, ordering)
    skel_skel = full_block[:, :SKEL, :SKEL]
    skel_red = full_block[:, :SKEL, SKEL:]
    red_skel = full_block[:, SKEL:, :SKEL]
    red_red = full_block[:, SKEL:, SKEL:]
    skel_interp = product("bij,bjk->bik", skel_skel, interp)
    x_skel_red = skel_red - skel_interp
    x_red_skel = red_skel - product("bji,bjk->bik", interp, skel_skel)
    x_red_red = red_red - product("bji,bjk->bik", interp, skel_red) - product("bij,bjk->bik", red_skel, interp)
    x_red_red = x_red_red + product("bji,bjk->bik", interp, skel_interp)
    identity = jnp.eye(RED, dtype=jnp.float32)
    diag_vals = jnp.diagonal(red_red, axis1=1, axis2=2)
    approx = identity[None] / diag_vals[:, None, :]
    for sweep_index in range(NS_ITERS):
        approx = 2.0 * approx - product("bij,bjk->bik", approx, product("bij,bjk->bik", x_red_red, approx))
    left_factor = product("bij,bjk->bik", x_skel_red, approx)
    right_factor = product("bij,bjk->bik", approx, x_red_skel)
    own_block = skel_skel - product("bij,bjk->bik", left_factor, x_red_skel)
    return approx, left_factor, right_factor, own_block


def slot_terms(near_piece, ordering, interp, approx, left_factor, right_factor):
    row_part = jnp.take_along_axis(near_piece[:, 0], ordering[:, None, :], axis=2)
    col_part = jnp.take_along_axis(near_piece[:, 1], ordering[:, None, :], axis=2)
    near_red = row_part[:, :, SKEL:] - product("bij,bjk->bik", row_part[:, :, :SKEL], interp)
    red_near_t = col_part[:, :, SKEL:] - product("bij,bjk->bik", col_part[:, :, :SKEL], interp)
    new_forward = jnp.swapaxes(col_part[:, :, :SKEL], 1, 2) - product("bij,bkj->bik", left_factor, red_near_t)
    new_backward = jnp.swapaxes(row_part[:, :, :SKEL], 1, 2) - product("bji,bkj->bik", right_factor, near_red)
    coupled = jnp.concatenate([new_forward, new_backward], axis=2)
    update = product("bij,bkj->bik", product("bij,bjk->bik", near_red, approx), red_near_t)
    return coupled, update


def reference(self_block, ordering, interp, near_band, pair_mask):
    offsets = [slot_index - REACH if slot_index < REACH else slot_index - REACH + 1 for slot_index in range(OFFS)]
    box_total = self_block.shape[0]
    groups = box_total // BOX_DEV

    def one_group(group_index):
        first_box = group_index * BOX_DEV
        box_ids = first_box + jnp.arange(BOX_DEV, dtype=jnp.int32)
        matrix = lax.dynamic_slice_in_dim(self_block, first_box, BOX_DEV, 0)
        order_part = lax.dynamic_slice_in_dim(ordering, first_box, BOX_DEV, 0)
        interp_part = lax.dynamic_slice_in_dim(interp, first_box, BOX_DEV, 0)
        approx, left_factor, right_factor, own_block = factors(matrix, order_part, interp_part)
        couples = []
        updates = []
        for slot_index in range(OFFS):
            source = ((box_ids - offsets[slot_index]) % box_total).astype(jnp.int32)
            weight = pair_mask[source, slot_index].astype(jnp.float32)
            near_piece = near_band[source, slot_index] * weight[:, None, None, None]
            coupled, update = slot_terms(near_piece, order_part, interp_part, approx, left_factor, right_factor)
            couples.append(coupled)
            updates.append(update)
        return own_block, approx, jnp.stack(couples, 1), jnp.stack(updates, 1)

    own_all, approx_all, couple_all, update_all = lax.map(one_group, jnp.arange(groups, dtype=jnp.int32))
    own_all = own_all.reshape(box_total, SKEL, SKEL)
    update_all = update_all.reshape(box_total, OFFS, SKEL, SKEL)
    summed = jnp.zeros_like(own_all)
    for slot_index in range(OFFS):
        summed = summed + jnp.roll(update_all[:, slot_index], -offsets[slot_index], axis=0)
    skeleton_self = own_all - summed
    red_inverse = approx_all.reshape(box_total, RED, RED)
    couplings = couple_all.reshape(box_total, OFFS, SKEL, 2 * SKEL)
    return skeleton_self, red_inverse, couplings
```

```python
import functools

import jax
import jax.numpy as jnp
from jax import lax
from jax.experimental import pallas as pl
from jax.experimental.pallas import tpu as pltpu
from jax.sharding import PartitionSpec as P

REACH = 4
NS_ITERS = 3
MESH = pl.DeviceIdType.MESH
NN = (((1,), (0,)), ((), ()))
NT = (((1,), (1,)), ((), ()))


def split(x):
    hi = x.astype(jnp.bfloat16)
    return hi, (x - hi.astype(jnp.float32)).astype(jnp.bfloat16)


def dot(a, b, dims=NN):
    return lax.dot_general(a, b, dims, preferred_element_type=jnp.float32)


def dot3(a, b, dims=NN):
    return dot(a[0], b[0], dims) + (dot(a[0], b[1], dims) + dot(a[1], b[0], dims))


def kernel(
    box_devs, nbr_devs, skel,
    self_ref, order_ref, interp_ref, band_ref, mask_ref,
    skel_out, inv_out, coup_out,
    blocks, bands, mask_far, y_buf, d_hi, d_lo, fac_hi, fac_lo, own, sums, arrived, others,
    a_own, a_send, a_recv, band_sem, band_send, mask_sem, u_sem, n_send, n_recv,
):
    boxes, rows, pts = self_ref.shape
    red = pts - skel
    slots = band_ref.shape[1]
    place = lax.axis_index("box")
    q = lax.axis_index("nbr")
    down = lax.rem(place + box_devs - 1, box_devs)
    up = lax.rem(place + 1, box_devs)
    first_half = q * slots < REACH
    pair, across, corner = (
        q + 1 - 2 * (q % 2),
        lax.rem(q + 2, 4),
        lax.rem(q + 2, 4) + 1 - 2 * (q % 2),
    )

    barrier = pltpu.get_barrier_semaphore()
    for other in (pair, across, corner):
        pl.semaphore_signal(barrier, inc=1, device_id=(place, other), device_id_type=MESH)
    for other in (down, up):
        pl.semaphore_signal(barrier, inc=1, device_id=(other, q), device_id_type=MESH)
    pl.semaphore_wait(barrier, 5)

    def my_rows(owner):
        return pl.ds(pl.multiple_of(owner * rows, rows), rows)

    def box_at(step):
        return jnp.where(first_half, boxes - 1 - step, step)

    def own_copy(b):
        return pltpu.make_async_copy(
            self_ref.at[b], blocks.at[b, my_rows(q)], a_own.at[b])

    def row_copy(b, kind, source_owner, target):
        src = self_ref.at[b] if kind < 2 else blocks.at[b, my_rows(source_owner)]
        return pltpu.make_async_remote_copy(
            src_ref=src, dst_ref=blocks.at[b, my_rows(source_owner)],
            send_sem=a_send.at[kind, b], recv_sem=a_recv.at[kind, b],
            device_id=(place, target), device_id_type=MESH)

    def row_wait(b, kind, source_owner):
        return pltpu.make_async_remote_copy(
            src_ref=blocks.at[b, my_rows(source_owner)],
            dst_ref=blocks.at[b, my_rows(source_owner)],
            send_sem=a_send.at[kind, b], recv_sem=a_recv.at[kind, b],
            device_id=(place, pair), device_id_type=MESH)

    far_device = jnp.where(first_half, down, up)
    near_device = jnp.where(first_half, up, down)

    def offset_of(s):
        slot = q * slots + s
        return jnp.where(slot < REACH, slot - REACH, slot - REACH + 1)

    mask_copy = pltpu.make_async_remote_copy(
        src_ref=mask_ref, dst_ref=mask_far, send_sem=mask_sem.at[0],
        recv_sem=mask_sem.at[1], device_id=(far_device, q), device_id_type=MESH)

    def band_far(b, s, source):
        return pltpu.make_async_remote_copy(
            src_ref=band_ref.at[source, s], dst_ref=bands.at[b, s],
            send_sem=band_send.at[b, s], recv_sem=band_sem.at[b, s],
            device_id=(far_device, q), device_id_type=MESH)

    def band_near(b, s, source):
        return pltpu.make_async_copy(
            band_ref.at[source, s], bands.at[b, s], band_sem.at[b, s])

    def is_far(b, s):
        c = b - offset_of(s)
        return (c < 0) | (c >= boxes)

    def source_of(b, s):
        return lax.rem(b - offset_of(s) + boxes, boxes)

    def start(step, carry):
        for_across = jnp.where(first_half, step, boxes - 1 - step)
        row_copy(for_across, 1, q, across).start()
        b = box_at(step)
        row_copy(b, 0, q, pair).start()
        own_copy(b).start()
        return carry

    mask_copy.start()
    lax.fori_loop(0, boxes, start, 0)

    def start_band(step, carry):
        b = box_at(step)
        for s in range(slots):
            @pl.when(is_far(b, s))
            def _():
                band_far(b, s, source_of(b, s)).start()

            @pl.when(jnp.logical_not(is_far(b, s)))
            def _():
                band_near(b, s, source_of(b, s)).start()
        return carry

    lax.fori_loop(0, boxes, start_band, 0)
    sums[...] = jnp.zeros_like(sums)

    lane = lax.broadcasted_iota(jnp.int32, (pts, pts), 1)
    sub = lax.broadcasted_iota(jnp.int32, (pts, pts), 0)
    on_diag = sub == lane
    red_diag = lax.broadcasted_iota(jnp.int32, (red, red), 0) == lax.broadcasted_iota(
        jnp.int32, (red, red), 1)

    def forward(b):
        row_wait(b, 1, across).wait_recv()
        row_copy(b, 2, across, pair).start()

    def factor(step, carry):
        b = box_at(step)

        @pl.when(step == 0)
        def _():
            forward(b)

        @pl.when(step + 1 < boxes)
        def _():
            forward(box_at(step + 1))

        order_row = order_ref[pl.ds(b, 1), :].astype(jnp.float32)
        order_col = jnp.broadcast_to(order_row, (8, pts)).T[:, 0:1].astype(jnp.int32)
        chosen = order_col == lane
        one_hot = jnp.where(chosen, 1.0, 0.0)
        t_hi, t_lo = split(interp_ref[b].T)
        skel_hot = one_hot[:skel].astype(jnp.bfloat16)
        spread_hi = dot(t_hi, skel_hot)
        spread_lo = dot(t_lo, skel_hot)
        d_hi[b] = jnp.concatenate([one_hot[:skel], one_hot[skel:] - spread_hi], 0).astype(jnp.bfloat16)
        d_lo[b] = -spread_lo.astype(jnp.bfloat16)
        dh, dl = d_hi[b], d_lo[b]

        own_copy(b).wait()
        row_wait(b, 0, pair).wait_recv()
        row_wait(b, 2, corner).wait_recv()
        matrix = blocks[b]
        diag_row = jnp.sum(jnp.where(on_diag, matrix, 0.0), axis=0, keepdims=True)
        diag_col = jnp.sum(jnp.where(chosen[skel:], diag_row, 0.0), axis=1, keepdims=True)
        inv_col = 1.0 / diag_col
        start_y = jnp.where(red_diag, inv_col, 0.0)
        inv_row = jnp.sum(start_y, axis=0, keepdims=True)

        m_hi, m_lo = split(matrix)
        left = dot(dh, m_hi) + dot(dh, m_lo)
        left = jnp.concatenate([left[:skel], left[skel:] + dot(dl, m_hi)], 0)
        v_hi, v_lo = split(left)
        right = dot(v_hi, dh, NT) + dot(v_lo, dh, NT)
        fix = dot(v_hi, dl, NT)
        skel_skel = right[:skel, :skel]
        x_sr = right[:skel, skel:] + fix[:skel]
        x_rs = right[skel:, :skel]
        x_rr = right[skel:, skel:] + fix[skel:]
        xrr = split(x_rr)
        y = 2.0 * start_y - inv_col * (x_rr * inv_row)
        for _ in range(NS_ITERS - 1):
            ys = split(y)
            y = 2.0 * y - dot3(ys, split(dot3(xrr, ys)))
        ys = split(y)
        xrs = split(x_rs)
        left_factor = dot3(split(x_sr), ys)
        right_factor = dot3(ys, xrs)
        lf = split(left_factor)
        own_block = skel_skel - dot3(lf, xrs)
        rt = split(right_factor.T)
        fac_hi[b] = jnp.concatenate([lf[0], rt[0], ys[0]], 0)
        fac_lo[b] = jnp.concatenate([lf[1], rt[1], ys[1]], 0)
        own[b] = own_block
        y_buf[...] = y
        part = red // nbr_devs
        inv_out[b] = y_buf[pl.ds(pl.multiple_of(q * part, 8), part)]
        return carry

    def done_sends(step, carry):
        b = box_at(step)
        row_copy(b, 2, across, pair).wait_send()
        row_copy(b, 1, q, across).wait_send()
        row_copy(b, 0, q, pair).wait_send()
        return carry

    lax.fori_loop(0, boxes, factor, 0)
    lax.fori_loop(0, boxes, done_sends, 0)
    mask_copy.wait()

    half = lax.rem(lax.broadcasted_iota(jnp.int32, (skel, slots * 2 * skel), 1), 2 * skel) < skel

    def slot_step(step, carry):
        b = box_at(step)
        pieces = []
        for s in range(slots):
            band_near(b, s, 0).wait()
            c = source_of(b, s)
            far = is_far(b, s).astype(jnp.int32)
            weight = far * mask_far[pl.ds(c, 1), s : s + 1] + (1 - far) * mask_ref[pl.ds(c, 1), s : s + 1]
            weight = weight.astype(jnp.float32)
            pieces += [bands[b, s, 1] * weight, bands[b, s, 0] * weight]
        b_hi, b_lo = split(jnp.concatenate(pieces, 0))
        dh, dl = d_hi[b], d_lo[b]
        turned = dot(dh, b_hi, NT) + dot(dh, b_lo, NT)
        skel_part = turned[:skel]
        red_part = turned[skel:] + dot(dl, b_hi, NT)
        f = dot3((fac_hi[b], fac_lo[b]), split(red_part))
        coupled = skel_part - jnp.where(half, f[:skel], f[skel : 2 * skel])
        flipped = red_part.T
        z = split(f[2 * skel :])
        near_red = split(jnp.concatenate(
            [flipped[(2 * s + 1) * skel : (2 * s + 2) * skel] for s in range(slots)], 0))
        u = dot3(near_red, z)
        for s in range(slots):
            coup_out[b, s] = coupled[:, 2 * s * skel : 2 * (s + 1) * skel]
            one = u[s * skel : (s + 1) * skel, 2 * s * skel : (2 * s + 1) * skel]
            packed = jnp.concatenate([one[: skel // 2], one[skel // 2 :]], 1)
            at = b - offset_of(s) + REACH
            sums[at] = sums[at] + packed
        return carry

    lax.fori_loop(0, REACH, slot_step, 0)
    leaving = jnp.where(first_half, boxes + REACH, 0)
    u_copy = pltpu.make_async_remote_copy(
        src_ref=sums.at[pl.ds(leaving, REACH)], dst_ref=arrived, send_sem=u_sem.at[0],
        recv_sem=u_sem.at[1], device_id=(near_device, q), device_id_type=MESH)
    u_copy.start()
    lax.fori_loop(REACH, boxes, slot_step, 0)
    u_copy.wait()
    landing = jnp.where(first_half, REACH, boxes)
    sums[pl.ds(landing, REACH)] = sums[pl.ds(landing, REACH)] + arrived[...]

    mine = sums.at[pl.ds(REACH, boxes)]
    copies = []
    for k, other in enumerate((pair, across, corner)):
        copies.append(pltpu.make_async_remote_copy(
            src_ref=mine, dst_ref=others.at[k], send_sem=n_send.at[k],
            recv_sem=n_recv.at[k], device_id=(place, other), device_id_type=MESH))
    for copy in copies:
        copy.start()

    def band_done(step, carry):
        b = box_at(step)
        for s in range(slots):
            @pl.when(is_far(b, s))
            def _():
                band_far(b, s, source_of(b, s)).wait_send()
        return carry

    lax.fori_loop(0, boxes, band_done, 0)
    for copy in copies:
        copy.wait()

    def finish(c, carry):
        total = (sums[c + REACH] + others[0, c]) + (others[1, c] + others[2, c])
        full = jnp.concatenate([total[:, :skel], total[:, skel:]], 0)
        skel_out[c] = own[c] - full
        return carry

    lax.fori_loop(0, boxes, finish, 0)


def body(box_devs, nbr_devs, self_block, ordering, interp, near_band, pair_mask):
    boxes, rows, pts = self_block.shape
    skel, red = interp.shape[1:]
    slots = near_band.shape[1]
    f32, bf16 = jnp.float32, jnp.bfloat16
    vmem = pl.BlockSpec(memory_space=pltpu.VMEM)
    hbm = pl.BlockSpec(memory_space=pl.ANY)
    dma = pltpu.SemaphoreType.DMA
    return pl.pallas_call(
        functools.partial(kernel, box_devs, nbr_devs, skel),
        out_shape=(
            jax.ShapeDtypeStruct((boxes, skel, skel), f32),
            jax.ShapeDtypeStruct((boxes, red // nbr_devs, red), f32),
            jax.ShapeDtypeStruct((boxes, slots, skel, 2 * skel), f32),
        ),
        in_specs=[hbm, vmem, vmem, hbm, vmem],
        out_specs=(vmem, vmem, vmem),
        scratch_shapes=[
            pltpu.VMEM((boxes, pts, pts), f32),
            pltpu.VMEM((boxes, slots, 2, skel, pts), f32),
            pltpu.VMEM(pair_mask.shape, jnp.int32),
            pltpu.VMEM((red, red), f32),
            pltpu.VMEM((boxes, pts, pts), bf16),
            pltpu.VMEM((boxes, red, pts), bf16),
            pltpu.VMEM((boxes, 2 * skel + red, red), bf16),
            pltpu.VMEM((boxes, 2 * skel + red, red), bf16),
            pltpu.VMEM((boxes, skel, skel), f32),
            pltpu.VMEM((boxes + 2 * REACH, skel // 2, 2 * skel), f32),
            pltpu.VMEM((REACH, skel // 2, 2 * skel), f32),
            pltpu.VMEM((nbr_devs - 1, boxes, skel // 2, 2 * skel), f32),
            dma((boxes,)),
            dma((3, boxes)),
            dma((3, boxes)),
            dma((boxes, slots)),
            dma((boxes, slots)),
            dma((2,)),
            dma((2,)),
            dma((nbr_devs - 1,)),
            dma((nbr_devs - 1,)),
        ],
        compiler_params=pltpu.CompilerParams(
            collective_id=0, has_side_effects=True, vmem_limit_bytes=56 * 1024 * 1024),
        name="level",
    )(self_block, ordering, interp, near_band, pair_mask)


def solution(mesh):
    placed = (
        P("box", "nbr", None),
        P("box", None),
        P("box", None, None),
        P("box", "nbr", None, None, None),
        P("box", "nbr"),
    )
    return jax.shard_map(
        functools.partial(body, mesh.shape["box"], mesh.shape["nbr"]),
        mesh=mesh,
        in_specs=placed,
        out_specs=(P("box", None, None), P("box", "nbr", None), P("box", "nbr", None, None)),
        check_vma=False,
    )
```

```python
import functools

import jax
import jax.numpy as jnp
from jax import lax
from jax.experimental import pallas as pl
from jax.experimental.pallas import tpu as pltpu
from jax.sharding import PartitionSpec as P

REACH = 4
NS_ITERS = 3
MESH = pl.DeviceIdType.MESH
NN = (((1,), (0,)), ((), ()))
NT = (((1,), (1,)), ((), ()))


def split(x):
    hi = x.astype(jnp.bfloat16)
    return hi, (x - hi.astype(jnp.float32)).astype(jnp.bfloat16)


def dot(a, b, dims=NN):
    return lax.dot_general(a, b, dims, preferred_element_type=jnp.float32)


def dot3(a, b, dims=NN):
    return dot(a[0], b[0], dims) + (dot(a[0], b[1], dims) + dot(a[1], b[0], dims))


def kernel(
    box_devs, nbr_devs, skel,
    self_ref, order_ref, interp_ref, band_ref, mask_ref,
    skel_out, inv_out, coup_out,
    blocks, bands, mask_far, y_buf, d_hi, d_lo, fac_hi, fac_lo, own, sums, arrived, others,
    a_own, a_send, a_recv, band_sem, band_send, mask_sem, u_sem, n_send, n_recv,
):
    boxes, rows, pts = self_ref.shape
    red = pts - skel
    slots = band_ref.shape[1]
    place = lax.axis_index("box")
    q = lax.axis_index("nbr")
    down = lax.rem(place + box_devs - 1, box_devs)
    up = lax.rem(place + 1, box_devs)
    first_half = q * slots < REACH
    pair, across, corner = (
        q + 1 - 2 * (q % 2),
        lax.rem(q + 2, 4),
        lax.rem(q + 2, 4) + 1 - 2 * (q % 2),
    )

    barrier = pltpu.get_barrier_semaphore()
    for other in (pair, across, corner):
        pl.semaphore_signal(barrier, inc=1, device_id=(place, other), device_id_type=MESH)
    for other in (down, up):
        pl.semaphore_signal(barrier, inc=1, device_id=(other, q), device_id_type=MESH)

    def my_rows(owner):
        return pl.ds(pl.multiple_of(owner * rows, rows), rows)

    def box_at(step):
        spot = jnp.where(step == 0, REACH, jnp.where(step <= REACH, step - 1, step))
        return jnp.where(first_half, boxes - 1 - spot, spot)

    def own_copy(b):
        return pltpu.make_async_copy(
            self_ref.at[b], blocks.at[b, my_rows(q)], a_own.at[b])

    def row_copy(b, kind, source_owner, target):
        src = self_ref.at[b] if kind < 2 else blocks.at[b, my_rows(source_owner)]
        return pltpu.make_async_remote_copy(
            src_ref=src, dst_ref=blocks.at[b, my_rows(source_owner)],
            send_sem=a_send.at[kind, b], recv_sem=a_recv.at[kind, b],
            device_id=(place, target), device_id_type=MESH)

    def row_wait(b, kind, source_owner):
        return pltpu.make_async_remote_copy(
            src_ref=blocks.at[b, my_rows(source_owner)],
            dst_ref=blocks.at[b, my_rows(source_owner)],
            send_sem=a_send.at[kind, b], recv_sem=a_recv.at[kind, b],
            device_id=(place, pair), device_id_type=MESH)

    far_device = jnp.where(first_half, down, up)
    near_device = jnp.where(first_half, up, down)

    def offset_of(s):
        slot = q * slots + s
        return jnp.where(slot < REACH, slot - REACH, slot - REACH + 1)

    mask_copy = pltpu.make_async_remote_copy(
        src_ref=mask_ref, dst_ref=mask_far, send_sem=mask_sem.at[0],
        recv_sem=mask_sem.at[1], device_id=(far_device, q), device_id_type=MESH)

    def band_far(b, s, source):
        return pltpu.make_async_remote_copy(
            src_ref=band_ref.at[source, s], dst_ref=bands.at[b, s],
            send_sem=band_send.at[b, s], recv_sem=band_sem.at[b, s],
            device_id=(far_device, q), device_id_type=MESH)

    def band_near(b, s, source):
        return pltpu.make_async_copy(
            band_ref.at[source, s], bands.at[b, s], band_sem.at[b, s])

    def is_far(b, s):
        c = b - offset_of(s)
        return (c < 0) | (c >= boxes)

    def source_of(b, s):
        return lax.rem(b - offset_of(s) + boxes, boxes)

    def start(step, carry):
        b = box_at(step)
        row_copy(boxes - 1 - b, 1, q, across).start()
        row_copy(b, 0, q, pair).start()
        return carry

    def start_near(step, carry):
        b = box_at(step)
        own_copy(b).start()
        for s in range(slots):
            @pl.when(jnp.logical_not(is_far(b, s)))
            def _():
                band_near(b, s, source_of(b, s)).start()
        return carry

    def start_far(step, carry):
        b = box_at(step)
        for s in range(slots):
            @pl.when(is_far(b, s))
            def _():
                band_far(b, s, source_of(b, s)).start()
        return carry

    lax.fori_loop(0, boxes, start_near, 0)
    sums[...] = jnp.zeros_like(sums)

    lane = lax.broadcasted_iota(jnp.int32, (pts, pts), 1)
    sub = lax.broadcasted_iota(jnp.int32, (pts, pts), 0)
    on_diag = sub == lane
    red_diag = lax.broadcasted_iota(jnp.int32, (red, red), 0) == lax.broadcasted_iota(
        jnp.int32, (red, red), 1)

    def forward(b):
        row_wait(b, 1, across).wait_recv()
        row_copy(b, 2, across, pair).start()

    def chosen_of(b):
        order_row = order_ref[pl.ds(b, 1), :].astype(jnp.float32)
        return jnp.broadcast_to(order_row, (8, pts)).T[:, 0:1].astype(jnp.int32) == lane

    def prepare(step, carry):
        b = box_at(step)
        one_hot = jnp.where(chosen_of(b), 1.0, 0.0)
        t_hi, t_lo = split(interp_ref[b].T)
        skel_hot = one_hot[:skel].astype(jnp.bfloat16)
        spread_hi = dot(t_hi, skel_hot)
        spread_lo = dot(t_lo, skel_hot)
        d_hi[b] = jnp.concatenate([one_hot[:skel], one_hot[skel:] - spread_hi], 0).astype(jnp.bfloat16)
        d_lo[b] = -spread_lo.astype(jnp.bfloat16)
        return carry

    def factor(step):
        b = box_at(step)
        dh, dl = d_hi[b], d_lo[b]
        chosen = chosen_of(b)
        own_copy(b).wait()
        row_wait(b, 0, pair).wait_recv()
        row_wait(b, 2, corner).wait_recv()
        matrix = blocks[b]
        diag_row = jnp.sum(jnp.where(on_diag, matrix, 0.0), axis=0, keepdims=True)
        diag_col = jnp.sum(jnp.where(chosen[skel:], diag_row, 0.0), axis=1, keepdims=True)
        inv_col = 1.0 / diag_col
        start_y = jnp.where(red_diag, inv_col, 0.0)
        inv_row = jnp.sum(start_y, axis=0, keepdims=True)

        m_hi, m_lo = split(matrix)
        left = dot(dh, m_hi) + dot(dh, m_lo)
        left = jnp.concatenate([left[:skel], left[skel:] + dot(dl, m_hi)], 0)
        v_hi, v_lo = split(left)
        right = dot(v_hi, dh, NT) + dot(v_lo, dh, NT)
        fix = dot(v_hi, dl, NT)
        skel_skel = right[:skel, :skel]
        x_sr = right[:skel, skel:] + fix[:skel]
        x_rs = right[skel:, :skel]
        x_rr = right[skel:, skel:] + fix[skel:]
        xrr = split(x_rr)
        y = 2.0 * start_y - inv_col * (x_rr * inv_row)
        for _ in range(NS_ITERS - 1):
            ys = split(y)
            y = 2.0 * y - dot3(ys, split(dot3(xrr, ys)))
        ys = split(y)
        xrs = split(x_rs)
        left_factor = dot3(split(x_sr), ys)
        right_factor = dot3(ys, xrs)
        lf = split(left_factor)
        own_block = skel_skel - dot3(lf, xrs)
        rt = split(right_factor.T)
        fac_hi[b] = jnp.concatenate([lf[0], rt[0], ys[0]], 0)
        fac_lo[b] = jnp.concatenate([lf[1], rt[1], ys[1]], 0)
        own[b] = own_block
        y_buf[...] = y
        part = red // nbr_devs
        inv_out[b] = y_buf[pl.ds(pl.multiple_of(q * part, 8), part)]

    def done_sends(step, carry):
        b = box_at(step)
        row_copy(b, 2, across, pair).wait_send()
        row_copy(b, 1, q, across).wait_send()
        row_copy(b, 0, q, pair).wait_send()
        return carry

    half = lax.rem(lax.broadcasted_iota(jnp.int32, (skel, slots * 2 * skel), 1), 2 * skel) < skel

    mask_lane = lax.broadcasted_iota(jnp.int32, (1, boxes), 1)

    def slot_step(step):
        b = box_at(step)
        pieces = []
        for s in range(slots):
            band_near(b, s, 0).wait()
            c = source_of(b, s)
            far = is_far(b, s).astype(jnp.int32)
            weight = far * mask_far[s : s + 1, :] + (1 - far) * mask_ref[s : s + 1, :]
            weight = jnp.sum(
                jnp.where(mask_lane == c, weight.astype(jnp.float32), 0.0), axis=1, keepdims=True)
            pieces += [bands[b, s, 1] * weight, bands[b, s, 0] * weight]
        b_hi, b_lo = split(jnp.concatenate(pieces, 0))
        dh, dl = d_hi[b], d_lo[b]
        turned = dot(dh, b_hi, NT) + dot(dh, b_lo, NT)
        skel_part = turned[:skel]
        red_part = turned[skel:] + dot(dl, b_hi, NT)
        f = dot3((fac_hi[b], fac_lo[b]), split(red_part))
        coupled = skel_part - jnp.where(half, f[:skel], f[skel : 2 * skel])
        flipped = red_part.T
        z = split(f[2 * skel :])
        near_red = split(jnp.concatenate(
            [flipped[(2 * s + 1) * skel : (2 * s + 2) * skel] for s in range(slots)], 0))
        u = dot3(near_red, z)
        for s in range(slots):
            coup_out[b, s] = coupled[:, 2 * s * skel : 2 * (s + 1) * skel]
            one = u[s * skel : (s + 1) * skel, 2 * s * skel : (2 * s + 1) * skel]
            packed = jnp.concatenate([one[: skel // 2], one[skel // 2 :]], 1)
            at = b - offset_of(s) + REACH
            sums[at] = sums[at] + packed

    leaving = jnp.where(first_half, boxes + REACH, 0)
    landing = jnp.where(first_half, REACH, boxes)
    u_copy = pltpu.make_async_remote_copy(
        src_ref=sums.at[pl.ds(leaving, REACH)], dst_ref=arrived, send_sem=u_sem.at[0],
        recv_sem=u_sem.at[1], device_id=(near_device, q), device_id_type=MESH)
    spans = [jnp.abs(offset_of(s)) for s in range(slots)]
    longest = functools.reduce(jnp.maximum, spans)
    shortest = functools.reduce(jnp.minimum, spans)
    peers = (across, corner, pair)

    def ready_at(c):
        seen = jnp.where(first_half, c, boxes - 1 - c)
        last = boxes - 1 - jnp.maximum(seen - longest, 0)
        last = jnp.where(seen >= shortest, jnp.maximum(last, REACH), REACH)
        return jnp.where(seen < REACH, jnp.maximum(last, boxes - 2), last)

    def sum_copy(k, c):
        return pltpu.make_async_remote_copy(
            src_ref=sums.at[c + REACH], dst_ref=others.at[k, c], send_sem=n_send.at[k, c],
            recv_sem=n_recv.at[k, c], device_id=(place, peers[k]), device_id_type=MESH)

    def main(step, carry):
        factor(step)

        @pl.when(step == 0)
        def _():
            forward(box_at(1))
            mask_copy.wait()

        slot_step(step)

        @pl.when(step + 2 < boxes)
        def _():
            forward(box_at(step + 2))

        @pl.when(step == REACH)
        def _():
            u_copy.start()

        @pl.when(step == boxes - 2)
        def _():
            u_copy.wait()
            sums[pl.ds(landing, REACH)] = sums[pl.ds(landing, REACH)] + arrived[...]

        def share(c, carry):
            @pl.when(ready_at(c) == step)
            def _():
                for k in range(len(peers)):
                    sum_copy(k, c).start()
            return carry

        @pl.when(step >= REACH)
        def _():
            lax.fori_loop(0, boxes, share, 0)

        return carry

    early = 3
    lax.fori_loop(0, early, prepare, 0)
    pl.semaphore_wait(barrier, 5)
    lax.fori_loop(0, boxes, start, 0)
    mask_copy.start()
    lax.fori_loop(0, boxes, start_far, 0)
    lax.fori_loop(early, boxes, prepare, 0)
    forward(box_at(0))
    lax.fori_loop(0, boxes, main, 0)
    lax.fori_loop(0, boxes, done_sends, 0)

    def band_done(step, carry):
        b = box_at(step)
        for s in range(slots):
            @pl.when(is_far(b, s))
            def _():
                band_far(b, s, source_of(b, s)).wait_send()
        return carry

    lax.fori_loop(0, boxes, band_done, 0)

    def finish(c, carry):
        for k in range(len(peers)):
            sum_copy(k, c).wait()
        total = (sums[c + REACH] + others[0, c]) + (others[1, c] + others[2, c])
        full = jnp.concatenate([total[:, :skel], total[:, skel:]], 0)
        skel_out[c] = own[c] - full
        return carry

    lax.fori_loop(0, boxes, finish, 0)


def deliver_kernel(count, *refs):
    sems = refs[-1]
    copies = [
        pltpu.make_async_copy(refs[n], refs[count + n], sems.at[n]) for n in range(count)]
    for copy in copies:
        copy.start()
    for copy in copies:
        copy.wait()


def deliver(arrays):
    anywhere = pl.BlockSpec(memory_space=pl.ANY)
    return pl.pallas_call(
        functools.partial(deliver_kernel, len(arrays)),
        out_shape=tuple(jax.ShapeDtypeStruct(a.shape, a.dtype) for a in arrays),
        in_specs=[anywhere] * len(arrays),
        out_specs=[anywhere] * len(arrays),
        scratch_shapes=[pltpu.SemaphoreType.DMA((len(arrays),))],
        compiler_params=pltpu.CompilerParams(vmem_limit_bytes=1024 * 1024),
        name="deliver",
    )(*arrays)


def body(box_devs, nbr_devs, self_block, ordering, interp, near_band, pair_mask):
    boxes, rows, pts = self_block.shape
    skel, red = interp.shape[1:]
    slots = near_band.shape[1]
    f32, bf16 = jnp.float32, jnp.bfloat16
    vmem = pl.BlockSpec(memory_space=pltpu.VMEM)
    hbm = pl.BlockSpec(memory_space=pltpu.HBM)
    dma = pltpu.SemaphoreType.DMA
    results = pl.pallas_call(
        functools.partial(kernel, box_devs, nbr_devs, skel),
        out_shape=(
            jax.ShapeDtypeStruct((boxes, skel, skel), f32),
            jax.ShapeDtypeStruct((boxes, red // nbr_devs, red), f32),
            jax.ShapeDtypeStruct((boxes, slots, skel, 2 * skel), f32),
        ),
        in_specs=[hbm, vmem, vmem, hbm, vmem],
        out_specs=(vmem, vmem, vmem),
        scratch_shapes=[
            pltpu.VMEM((boxes, pts, pts), f32),
            pltpu.VMEM((boxes, slots, 2, skel, pts), f32),
            pltpu.VMEM(pair_mask.shape[::-1], jnp.int32),
            pltpu.VMEM((red, red), f32),
            pltpu.VMEM((boxes, pts, pts), bf16),
            pltpu.VMEM((boxes, red, pts), bf16),
            pltpu.VMEM((boxes, 2 * skel + red, red), bf16),
            pltpu.VMEM((boxes, 2 * skel + red, red), bf16),
            pltpu.VMEM((boxes, skel, skel), f32),
            pltpu.VMEM((boxes + 2 * REACH, skel // 2, 2 * skel), f32),
            pltpu.VMEM((REACH, skel // 2, 2 * skel), f32),
            pltpu.VMEM((nbr_devs - 1, boxes, skel // 2, 2 * skel), f32),
            dma((boxes,)),
            dma((3, boxes)),
            dma((3, boxes)),
            dma((boxes, slots)),
            dma((boxes, slots)),
            dma((2,)),
            dma((2,)),
            dma((nbr_devs - 1, boxes)),
            dma((nbr_devs - 1, boxes)),
        ],
        compiler_params=pltpu.CompilerParams(
            collective_id=0, has_side_effects=True, vmem_limit_bytes=52 * 1024 * 1024),
        name="level",
    )(self_block, ordering, interp, near_band, pair_mask.T)
    return deliver(results)


def solution(mesh):
    placed = (
        P("box", "nbr", None),
        P("box", None),
        P("box", None, None),
        P("box", "nbr", None, None, None),
        P("box", "nbr"),
    )
    return jax.shard_map(
        functools.partial(body, mesh.shape["box"], mesh.shape["nbr"]),
        mesh=mesh,
        in_specs=placed,
        out_specs=(P("box", None, None), P("box", "nbr", None), P("box", "nbr", None, None)),
        check_vma=False,
    )
```

```python
import functools

import jax
import jax.numpy as jnp
from jax import lax
from jax.experimental import pallas as pl
from jax.experimental.pallas import tpu as pltpu
from jax.sharding import PartitionSpec as P

REACH = 4
NS_ITERS = 3
MESH = pl.DeviceIdType.MESH
NN = (((1,), (0,)), ((), ()))
NT = (((1,), (1,)), ((), ()))


def split(x):
    hi = x.astype(jnp.bfloat16)
    return hi, (x - hi.astype(jnp.float32)).astype(jnp.bfloat16)


def dot(a, b, dims=NN):
    return lax.dot_general(a, b, dims, preferred_element_type=jnp.float32)


def dot3(a, b, dims=NN):
    return dot(a[0], b[0], dims) + (dot(a[0], b[1], dims) + dot(a[1], b[0], dims))


def kernel(
    box_devs, nbr_devs, skel,
    self_ref, order_ref, interp_ref, band_ref, mask_ref,
    skel_out, inv_out, coup_out,
    blocks, bands, mask_far, y_buf, d_hi, d_lo, fac_hi, fac_lo, own, sums, arrived, others,
    a_own, a_send, a_recv, band_sem, band_send, mask_sem, u_sem, n_send, n_recv,
):
    boxes, rows, pts = self_ref.shape
    red = pts - skel
    slots = band_ref.shape[1]
    place = lax.axis_index("box")
    q = lax.axis_index("nbr")
    down = lax.rem(place + box_devs - 1, box_devs)
    up = lax.rem(place + 1, box_devs)
    first_half = q * slots < REACH
    pair, across, corner = (
        q + 1 - 2 * (q % 2),
        lax.rem(q + 2, 4),
        lax.rem(q + 2, 4) + 1 - 2 * (q % 2),
    )

    barrier = pltpu.get_barrier_semaphore()
    for other in (pair, across, corner):
        pl.semaphore_signal(barrier, inc=1, device_id=(place, other), device_id_type=MESH)
    for other in (down, up):
        pl.semaphore_signal(barrier, inc=1, device_id=(other, q), device_id_type=MESH)

    def my_rows(owner):
        return pl.ds(pl.multiple_of(owner * rows, rows), rows)

    def box_at(step):
        return jnp.where(first_half, boxes - 1 - step, step)

    def own_copy(b):
        return pltpu.make_async_copy(
            self_ref.at[b], blocks.at[b, my_rows(q)], a_own.at[b])

    def row_copy(b, kind, source_owner, target):
        src = self_ref.at[b] if kind < 2 else blocks.at[b, my_rows(source_owner)]
        return pltpu.make_async_remote_copy(
            src_ref=src, dst_ref=blocks.at[b, my_rows(source_owner)],
            send_sem=a_send.at[kind, b], recv_sem=a_recv.at[kind, b],
            device_id=(place, target), device_id_type=MESH)

    def row_wait(b, kind, source_owner):
        return pltpu.make_async_remote_copy(
            src_ref=blocks.at[b, my_rows(source_owner)],
            dst_ref=blocks.at[b, my_rows(source_owner)],
            send_sem=a_send.at[kind, b], recv_sem=a_recv.at[kind, b],
            device_id=(place, pair), device_id_type=MESH)

    far_device = jnp.where(first_half, down, up)
    near_device = jnp.where(first_half, up, down)

    def offset_of(s):
        slot = q * slots + s
        return jnp.where(slot < REACH, slot - REACH, slot - REACH + 1)

    mask_copy = pltpu.make_async_remote_copy(
        src_ref=mask_ref, dst_ref=mask_far, send_sem=mask_sem.at[0],
        recv_sem=mask_sem.at[1], device_id=(far_device, q), device_id_type=MESH)

    def band_far(b, s, source):
        return pltpu.make_async_remote_copy(
            src_ref=band_ref.at[source, s], dst_ref=bands.at[b, s],
            send_sem=band_send.at[b, s], recv_sem=band_sem.at[b, s],
            device_id=(far_device, q), device_id_type=MESH)

    def band_near(b, s, source):
        return pltpu.make_async_copy(
            band_ref.at[source, s], bands.at[b, s], band_sem.at[b, s])

    def is_far(b, s):
        c = b - offset_of(s)
        return (c < 0) | (c >= boxes)

    def source_of(b, s):
        return lax.rem(b - offset_of(s) + boxes, boxes)

    def start(step, carry):
        b = box_at(step)
        row_copy(boxes - 1 - b, 1, q, across).start()
        row_copy(b, 0, q, pair).start()
        return carry

    def start_near(step, carry):
        b = box_at(step)
        own_copy(b).start()
        for s in range(slots):
            @pl.when(jnp.logical_not(is_far(b, s)))
            def _():
                band_near(b, s, source_of(b, s)).start()
        return carry

    def start_far(step, carry):
        b = box_at(step)
        for s in range(slots):
            @pl.when(is_far(b, s))
            def _():
                band_far(b, s, source_of(b, s)).start()
        return carry

    lax.fori_loop(0, boxes, start_near, 0)
    sums[...] = jnp.zeros_like(sums)

    lane = lax.broadcasted_iota(jnp.int32, (pts, pts), 1)
    sub = lax.broadcasted_iota(jnp.int32, (pts, pts), 0)
    on_diag = sub == lane
    red_diag = lax.broadcasted_iota(jnp.int32, (red, red), 0) == lax.broadcasted_iota(
        jnp.int32, (red, red), 1)

    def forward(b):
        row_wait(b, 1, across).wait_recv()
        row_copy(b, 2, across, pair).start()

    def chosen_of(b):
        order_row = order_ref[pl.ds(b, 1), :].astype(jnp.float32)
        return jnp.broadcast_to(order_row, (8, pts)).T[:, 0:1].astype(jnp.int32) == lane

    def prepare(step, carry):
        b = box_at(step)
        one_hot = jnp.where(chosen_of(b), 1.0, 0.0)
        t_hi, t_lo = split(interp_ref[b].T)
        skel_hot = one_hot[:skel].astype(jnp.bfloat16)
        spread_hi = dot(t_hi, skel_hot)
        spread_lo = dot(t_lo, skel_hot)
        d_hi[b] = jnp.concatenate([one_hot[:skel], one_hot[skel:] - spread_hi], 0).astype(jnp.bfloat16)
        d_lo[b] = -spread_lo.astype(jnp.bfloat16)
        return carry

    def each(f, *lists):
        return [f(*items) for items in zip(*lists)]

    def factor(bs):
        dh = [d_hi[b] for b in bs]
        dl = [d_lo[b] for b in bs]
        for b in bs:
            own_copy(b).wait()
            row_wait(b, 0, pair).wait_recv()
            row_wait(b, 2, corner).wait_recv()
        matrix = [blocks[b] for b in bs]
        ms = each(split, matrix)
        left = each(lambda d, m: dot(d, m[0]) + dot(d, m[1]), dh, ms)
        left = each(lambda l, d, m: jnp.concatenate(
            [l[:skel], l[skel:] + dot(d, m[0])], 0), left, dl, ms)
        vs = each(split, left)
        right = each(lambda v, d: dot(v[0], d, NT) + dot(v[1], d, NT), vs, dh)
        fix = each(lambda v, d: dot(v[0], d, NT), vs, dl)
        x_rr = each(lambda r, f: r[skel:, skel:] + f[skel:], right, fix)
        xrr = each(split, x_rr)
        y = []
        for n, b in enumerate(bs):
            diag_row = jnp.sum(jnp.where(on_diag, matrix[n], 0.0), axis=0, keepdims=True)
            diag_col = jnp.sum(
                jnp.where(chosen_of(b)[skel:], diag_row, 0.0), axis=1, keepdims=True)
            inv_col = 1.0 / diag_col
            start_y = jnp.where(red_diag, inv_col, 0.0)
            inv_row = jnp.sum(start_y, axis=0, keepdims=True)
            y.append(2.0 * start_y - inv_col * (x_rr[n] * inv_row))
        ys = each(split, y)
        for _ in range(NS_ITERS - 1):
            xy = each(split, each(dot3, xrr, ys))
            y = each(lambda a, p: 2.0 * a - p, y, each(dot3, ys, xy))
            ys = each(split, y)
        xrs = each(lambda r: split(r[skel:, :skel]), right)
        xsr = each(lambda r, f: split(r[:skel, skel:] + f[:skel]), right, fix)
        rt = each(lambda a, x: split(dot3(a, x).T), ys, xrs)
        lf = each(split, each(dot3, xsr, ys))
        owned = each(lambda r, l, x: r[:skel, :skel] - dot3(l, x), right, lf, xrs)
        part = red // nbr_devs
        for n, b in enumerate(bs):
            own[b] = owned[n]
            fac_hi[b] = jnp.concatenate([lf[n][0], rt[n][0], ys[n][0]], 0)
            fac_lo[b] = jnp.concatenate([lf[n][1], rt[n][1], ys[n][1]], 0)
            y_buf[n] = y[n]
        for n, b in enumerate(bs):
            inv_out[b] = y_buf[n, pl.ds(pl.multiple_of(q * part, 8), part)]

    def done_sends(step, carry):
        b = box_at(step)
        row_copy(b, 2, across, pair).wait_send()
        row_copy(b, 1, q, across).wait_send()
        row_copy(b, 0, q, pair).wait_send()
        return carry

    half = lax.rem(lax.broadcasted_iota(jnp.int32, (skel, slots * 2 * skel), 1), 2 * skel) < skel

    mask_lane = lax.broadcasted_iota(jnp.int32, (1, boxes), 1)

    def slot_step(bs):
        stacked = []
        for b in bs:
            pieces = []
            for s in range(slots):
                band_near(b, s, 0).wait()
                c = source_of(b, s)
                far = is_far(b, s).astype(jnp.int32)
                weight = far * mask_far[s : s + 1, :] + (1 - far) * mask_ref[s : s + 1, :]
                weight = jnp.sum(
                    jnp.where(mask_lane == c, weight.astype(jnp.float32), 0.0),
                    axis=1, keepdims=True)
                pieces += [bands[b, s, 1] * weight, bands[b, s, 0] * weight]
            stacked.append(split(jnp.concatenate(pieces, 0)))
        dh = [d_hi[b] for b in bs]
        dl = [d_lo[b] for b in bs]
        turned = each(lambda d, p: dot(d, p[0], NT) + dot(d, p[1], NT), dh, stacked)
        red_part = each(lambda t, d, p: t[skel:] + dot(d, p[0], NT), turned, dl, stacked)
        reds = each(split, red_part)
        f = each(lambda b, r: dot3((fac_hi[b], fac_lo[b]), r), bs, reds)
        near_red = each(lambda r: split(jnp.concatenate(
            [r[:, (2 * s + 1) * skel : (2 * s + 2) * skel] for s in range(slots)], 1).T), red_part)
        zs = each(lambda a: split(a[2 * skel :]), f)
        u = each(dot3, near_red, zs)
        for n, b in enumerate(bs):
            coupled = turned[n][:skel] - jnp.where(half, f[n][:skel], f[n][skel : 2 * skel])
            for s in range(slots):
                coup_out[b, s] = coupled[:, 2 * s * skel : 2 * (s + 1) * skel]
                one = u[n][s * skel : (s + 1) * skel, 2 * s * skel : (2 * s + 1) * skel]
                packed = jnp.concatenate([one[: skel // 2], one[skel // 2 :]], 1)
                at = b - offset_of(s) + REACH
                sums[at] = sums[at] + packed

    leaving = jnp.where(first_half, boxes + REACH, 0)
    landing = jnp.where(first_half, REACH, boxes)
    u_copy = pltpu.make_async_remote_copy(
        src_ref=sums.at[pl.ds(leaving, REACH)], dst_ref=arrived, send_sem=u_sem.at[0],
        recv_sem=u_sem.at[1], device_id=(near_device, q), device_id_type=MESH)
    spans = [jnp.abs(offset_of(s)) for s in range(slots)]
    longest = functools.reduce(jnp.maximum, spans)
    shortest = functools.reduce(jnp.minimum, spans)
    peers = (across, corner, pair)

    def ready_at(c):
        seen = jnp.where(first_half, c, boxes - 1 - c)
        last = boxes - 1 - jnp.maximum(seen - longest, 0)
        last = jnp.where(seen >= shortest, last, 0)
        return jnp.where(seen < REACH, jnp.maximum(last, boxes - 3), last) // 2

    def sum_copy(k, c):
        return pltpu.make_async_remote_copy(
            src_ref=sums.at[c + REACH], dst_ref=others.at[k, c], send_sem=n_send.at[k, c],
            recv_sem=n_recv.at[k, c], device_id=(place, peers[k]), device_id_type=MESH)

    def main(trip, carry):
        bs = [box_at(2 * trip), box_at(2 * trip + 1)]
        factor(bs)

        @pl.when(trip == 0)
        def _():
            mask_copy.wait()

        @pl.when(trip + 1 < boxes // 2)
        def _():
            forward(box_at(2 * trip + 2))
            forward(box_at(2 * trip + 3))

        slot_step(bs)

        @pl.when(trip == REACH // 2 - 1)
        def _():
            u_copy.start()

        @pl.when(trip == (boxes - 3) // 2)
        def _():
            u_copy.wait()
            sums[pl.ds(landing, REACH)] = sums[pl.ds(landing, REACH)] + arrived[...]

        def share(c, carry):
            @pl.when(ready_at(c) == trip)
            def _():
                for k in range(len(peers)):
                    sum_copy(k, c).start()
            return carry

        lax.fori_loop(0, boxes, share, 0)
        return carry

    early = 3
    lax.fori_loop(0, early, prepare, 0)
    pl.semaphore_wait(barrier, 5)
    lax.fori_loop(0, boxes, start, 0)
    mask_copy.start()
    lax.fori_loop(0, boxes, start_far, 0)
    lax.fori_loop(early, boxes, prepare, 0)
    forward(box_at(0))
    forward(box_at(1))
    lax.fori_loop(0, boxes // 2, main, 0)
    lax.fori_loop(0, boxes, done_sends, 0)

    def band_done(step, carry):
        b = box_at(step)
        for s in range(slots):
            @pl.when(is_far(b, s))
            def _():
                band_far(b, s, source_of(b, s)).wait_send()
        return carry

    lax.fori_loop(0, boxes, band_done, 0)

    def finish(c, carry):
        for k in range(len(peers)):
            sum_copy(k, c).wait()
        total = (sums[c + REACH] + others[0, c]) + (others[1, c] + others[2, c])
        full = jnp.concatenate([total[:, :skel], total[:, skel:]], 0)
        skel_out[c] = own[c] - full
        return carry

    lax.fori_loop(0, boxes, finish, 0)


def deliver_kernel(count, *refs):
    sems = refs[-1]
    copies = [
        pltpu.make_async_copy(refs[n], refs[count + n], sems.at[n]) for n in range(count)]
    for copy in copies:
        copy.start()
    for copy in copies:
        copy.wait()


def deliver(arrays):
    anywhere = pl.BlockSpec(memory_space=pl.ANY)
    return pl.pallas_call(
        functools.partial(deliver_kernel, len(arrays)),
        out_shape=tuple(jax.ShapeDtypeStruct(a.shape, a.dtype) for a in arrays),
        in_specs=[anywhere] * len(arrays),
        out_specs=[anywhere] * len(arrays),
        scratch_shapes=[pltpu.SemaphoreType.DMA((len(arrays),))],
        compiler_params=pltpu.CompilerParams(vmem_limit_bytes=1024 * 1024),
        name="deliver",
    )(*arrays)


def body(box_devs, nbr_devs, self_block, ordering, interp, near_band, pair_mask):
    boxes, rows, pts = self_block.shape
    skel, red = interp.shape[1:]
    slots = near_band.shape[1]
    f32, bf16 = jnp.float32, jnp.bfloat16
    vmem = pl.BlockSpec(memory_space=pltpu.VMEM)
    hbm = pl.BlockSpec(memory_space=pltpu.HBM)
    dma = pltpu.SemaphoreType.DMA
    results = pl.pallas_call(
        functools.partial(kernel, box_devs, nbr_devs, skel),
        out_shape=(
            jax.ShapeDtypeStruct((boxes, skel, skel), f32),
            jax.ShapeDtypeStruct((boxes, red // nbr_devs, red), f32),
            jax.ShapeDtypeStruct((boxes, slots, skel, 2 * skel), f32),
        ),
        in_specs=[hbm, vmem, vmem, hbm, vmem],
        out_specs=(vmem, vmem, vmem),
        scratch_shapes=[
            pltpu.VMEM((boxes, pts, pts), f32),
            pltpu.VMEM((boxes, slots, 2, skel, pts), f32),
            pltpu.VMEM(pair_mask.shape[::-1], jnp.int32),
            pltpu.VMEM((2, red, red), f32),
            pltpu.VMEM((boxes, pts, pts), bf16),
            pltpu.VMEM((boxes, red, pts), bf16),
            pltpu.VMEM((boxes, 2 * skel + red, red), bf16),
            pltpu.VMEM((boxes, 2 * skel + red, red), bf16),
            pltpu.VMEM((boxes, skel, skel), f32),
            pltpu.VMEM((boxes + 2 * REACH, skel // 2, 2 * skel), f32),
            pltpu.VMEM((REACH, skel // 2, 2 * skel), f32),
            pltpu.VMEM((nbr_devs - 1, boxes, skel // 2, 2 * skel), f32),
            dma((boxes,)),
            dma((3, boxes)),
            dma((3, boxes)),
            dma((boxes, slots)),
            dma((boxes, slots)),
            dma((2,)),
            dma((2,)),
            dma((nbr_devs - 1, boxes)),
            dma((nbr_devs - 1, boxes)),
        ],
        compiler_params=pltpu.CompilerParams(
            collective_id=0, has_side_effects=True, vmem_limit_bytes=52 * 1024 * 1024),
        name="level",
    )(self_block, ordering, interp, near_band, pair_mask.T)
    return deliver(results)


def solution(mesh):
    placed = (
        P("box", "nbr", None),
        P("box", None),
        P("box", None, None),
        P("box", "nbr", None, None, None),
        P("box", "nbr"),
    )
    return jax.shard_map(
        functools.partial(body, mesh.shape["box"], mesh.shape["nbr"]),
        mesh=mesh,
        in_specs=placed,
        out_specs=(P("box", None, None), P("box", "nbr", None), P("box", "nbr", None, None)),
        check_vma=False,
    )
```

```python
import functools

import jax
import jax.numpy as jnp
from jax import lax
from jax.experimental import pallas as pl
from jax.experimental.pallas import tpu as pltpu
from jax.sharding import PartitionSpec as P

REACH = 4
NS_ITERS = 3
MESH = pl.DeviceIdType.MESH
NN = (((1,), (0,)), ((), ()))
NT = (((1,), (1,)), ((), ()))


def split(x):
    hi = x.astype(jnp.bfloat16)
    return hi, (x - hi.astype(jnp.float32)).astype(jnp.bfloat16)


def dot(a, b, dims=NN):
    return lax.dot_general(a, b, dims, preferred_element_type=jnp.float32)


def dot3(a, b, dims=NN):
    return dot(a[0], b[0], dims) + (dot(a[0], b[1], dims) + dot(a[1], b[0], dims))


def kernel(
    box_devs, nbr_devs, skel,
    self_ref, order_ref, interp_ref, band_ref, mask_ref,
    skel_out, inv_out, coup_out,
    blocks, bands, mask_far, y_buf, d_hi, d_lo, fac_hi, fac_lo, own, sums, arrived, others,
    a_own, a_send, a_recv, band_sem, band_send, mask_sem, u_sem, n_send, n_recv,
):
    boxes, rows, pts = self_ref.shape
    red = pts - skel
    slots = band_ref.shape[1]
    place = lax.axis_index("box")
    q = lax.axis_index("nbr")
    down = lax.rem(place + box_devs - 1, box_devs)
    up = lax.rem(place + 1, box_devs)
    first_half = q * slots < REACH
    pair, across, corner = (
        q + 1 - 2 * (q % 2),
        lax.rem(q + 2, 4),
        lax.rem(q + 2, 4) + 1 - 2 * (q % 2),
    )

    barrier = pltpu.get_barrier_semaphore()
    for other in (pair, across, corner):
        pl.semaphore_signal(barrier, inc=1, device_id=(place, other), device_id_type=MESH)
    for other in (down, up):
        pl.semaphore_signal(barrier, inc=1, device_id=(other, q), device_id_type=MESH)

    def my_rows(owner):
        return pl.ds(pl.multiple_of(owner * rows, rows), rows)

    def box_at(step):
        return jnp.where(first_half, boxes - 1 - step, step)

    def own_copy(b):
        return pltpu.make_async_copy(
            self_ref.at[b], blocks.at[b, my_rows(q)], a_own.at[b])

    def row_copy(b, kind, source_owner, target):
        src = self_ref.at[b] if kind < 2 else blocks.at[b, my_rows(source_owner)]
        return pltpu.make_async_remote_copy(
            src_ref=src, dst_ref=blocks.at[b, my_rows(source_owner)],
            send_sem=a_send.at[kind, b], recv_sem=a_recv.at[kind, b],
            device_id=(place, target), device_id_type=MESH)

    def row_wait(b, kind, source_owner):
        return pltpu.make_async_remote_copy(
            src_ref=blocks.at[b, my_rows(source_owner)],
            dst_ref=blocks.at[b, my_rows(source_owner)],
            send_sem=a_send.at[kind, b], recv_sem=a_recv.at[kind, b],
            device_id=(place, pair), device_id_type=MESH)

    far_device = jnp.where(first_half, down, up)
    near_device = jnp.where(first_half, up, down)

    def offset_of(s):
        slot = q * slots + s
        return jnp.where(slot < REACH, slot - REACH, slot - REACH + 1)

    mask_copy = pltpu.make_async_remote_copy(
        src_ref=mask_ref, dst_ref=mask_far, send_sem=mask_sem.at[0],
        recv_sem=mask_sem.at[1], device_id=(far_device, q), device_id_type=MESH)

    def band_far(b, s, source):
        return pltpu.make_async_remote_copy(
            src_ref=band_ref.at[source, s], dst_ref=bands.at[b, s],
            send_sem=band_send.at[b, s], recv_sem=band_sem.at[b, s],
            device_id=(far_device, q), device_id_type=MESH)

    def band_near(b, s, source):
        return pltpu.make_async_copy(
            band_ref.at[source, s], bands.at[b, s], band_sem.at[b, s])

    def is_far(b, s):
        c = b - offset_of(s)
        return (c < 0) | (c >= boxes)

    def source_of(b, s):
        return lax.rem(b - offset_of(s) + boxes, boxes)

    def start(step, carry):
        b = box_at(step)
        row_copy(boxes - 1 - b, 1, q, across).start()
        row_copy(b, 0, q, pair).start()
        return carry

    def start_near(step, carry):
        b = box_at(step)
        own_copy(b).start()
        for s in range(slots):
            @pl.when(jnp.logical_not(is_far(b, s)))
            def _():
                band_near(b, s, source_of(b, s)).start()
        return carry

    def start_far(step, carry):
        b = box_at(step)
        for s in range(slots):
            @pl.when(is_far(b, s))
            def _():
                band_far(b, s, source_of(b, s)).start()
        return carry

    lax.fori_loop(0, boxes, start_near, 0)
    sums[...] = jnp.zeros_like(sums)

    lane = lax.broadcasted_iota(jnp.int32, (pts, pts), 1)
    sub = lax.broadcasted_iota(jnp.int32, (pts, pts), 0)
    on_diag = sub == lane
    red_diag = lax.broadcasted_iota(jnp.int32, (red, red), 0) == lax.broadcasted_iota(
        jnp.int32, (red, red), 1)

    def forward(b):
        row_wait(b, 1, across).wait_recv()
        row_copy(b, 2, across, pair).start()

    def chosen_of(b):
        order_row = order_ref[pl.ds(b, 1), :].astype(jnp.float32)
        return jnp.broadcast_to(order_row, (8, pts)).T[:, 0:1].astype(jnp.int32) == lane

    def prepare(step, carry):
        b = box_at(step)
        one_hot = jnp.where(chosen_of(b), 1.0, 0.0)
        t_hi, t_lo = split(interp_ref[b].T)
        skel_hot = one_hot[:skel].astype(jnp.bfloat16)
        spread_hi = dot(t_hi, skel_hot)
        spread_lo = dot(t_lo, skel_hot)
        d_hi[b] = jnp.concatenate([one_hot[:skel], one_hot[skel:] - spread_hi], 0).astype(jnp.bfloat16)
        d_lo[b] = -spread_lo.astype(jnp.bfloat16)
        return carry

    def each(f, *lists):
        return [f(*items) for items in zip(*lists)]

    def factor(bs):
        dh = [d_hi[b] for b in bs]
        dl = [d_lo[b] for b in bs]
        for b in bs:
            own_copy(b).wait()
            row_wait(b, 0, pair).wait_recv()
            row_wait(b, 2, corner).wait_recv()
        matrix = [blocks[b] for b in bs]
        ms = each(split, matrix)
        left = each(lambda d, m: dot(d, m[0]) + dot(d, m[1]), dh, ms)
        left = each(lambda l, d, m: jnp.concatenate(
            [l[:skel], l[skel:] + dot(d, m[0])], 0), left, dl, ms)
        vs = each(split, left)
        right = each(lambda v, d: dot(v[0], d, NT) + dot(v[1], d, NT), vs, dh)
        fix = each(lambda v, d: dot(v[0], d, NT), vs, dl)
        x_rr = each(lambda r, f: r[skel:, skel:] + f[skel:], right, fix)
        xrr = each(split, x_rr)
        y = []
        for n, b in enumerate(bs):
            diag_row = jnp.sum(jnp.where(on_diag, matrix[n], 0.0), axis=0, keepdims=True)
            diag_col = jnp.sum(
                jnp.where(chosen_of(b)[skel:], diag_row, 0.0), axis=1, keepdims=True)
            inv_col = 1.0 / diag_col
            start_y = jnp.where(red_diag, inv_col, 0.0)
            inv_row = jnp.sum(start_y, axis=0, keepdims=True)
            y.append(2.0 * start_y - inv_col * (x_rr[n] * inv_row))
        ys = each(split, y)
        for _ in range(NS_ITERS - 1):
            xy = each(split, each(dot3, xrr, ys))
            y = each(lambda a, p: 2.0 * a - p, y, each(dot3, ys, xy))
            ys = each(split, y)
        xrs = each(lambda r: split(r[skel:, :skel]), right)
        xsr = each(lambda r, f: split(r[:skel, skel:] + f[:skel]), right, fix)
        rt = each(lambda a, x: split(dot3(a, x).T), ys, xrs)
        lf = each(split, each(dot3, xsr, ys))
        owned = each(lambda r, l, x: r[:skel, :skel] - dot3(l, x), right, lf, xrs)
        part = red // nbr_devs
        for n, b in enumerate(bs):
            own[b] = owned[n]
            fac_hi[b] = jnp.concatenate([lf[n][0], rt[n][0], ys[n][0]], 0)
            fac_lo[b] = jnp.concatenate([lf[n][1], rt[n][1], ys[n][1]], 0)
            y_buf[n] = y[n]
        for n, b in enumerate(bs):
            inv_out[b] = y_buf[n, pl.ds(pl.multiple_of(q * part, 8), part)]

    def done_sends(step, carry):
        b = box_at(step)
        row_copy(b, 2, across, pair).wait_send()
        row_copy(b, 1, q, across).wait_send()
        row_copy(b, 0, q, pair).wait_send()
        return carry

    half = lax.rem(lax.broadcasted_iota(jnp.int32, (skel, slots * 2 * skel), 1), 2 * skel) < skel

    mask_lane = lax.broadcasted_iota(jnp.int32, (1, boxes), 1)

    def slot_step(bs):
        stacked = []
        for b in bs:
            pieces = []
            for s in range(slots):
                band_near(b, s, 0).wait()
                c = source_of(b, s)
                far = is_far(b, s).astype(jnp.int32)
                weight = far * mask_far[s : s + 1, :] + (1 - far) * mask_ref[s : s + 1, :]
                weight = jnp.sum(
                    jnp.where(mask_lane == c, weight.astype(jnp.float32), 0.0),
                    axis=1, keepdims=True)
                pieces += [bands[b, s, 1] * weight, bands[b, s, 0] * weight]
            stacked.append(split(jnp.concatenate(pieces, 0)))
        dh = [d_hi[b] for b in bs]
        dl = [d_lo[b] for b in bs]
        turned = each(lambda d, p: dot(d, p[0], NT) + dot(d, p[1], NT), dh, stacked)
        red_part = each(lambda t, d, p: t[skel:] + dot(d, p[0], NT), turned, dl, stacked)
        reds = each(split, red_part)
        f = each(lambda b, r: dot3((fac_hi[b], fac_lo[b]), r), bs, reds)
        near_red = each(lambda r: split(jnp.concatenate(
            [r[:, (2 * s + 1) * skel : (2 * s + 2) * skel] for s in range(slots)], 1).T), red_part)
        zs = each(lambda a: split(a[2 * skel :]), f)
        u = each(dot3, near_red, zs)
        for n, b in enumerate(bs):
            coupled = turned[n][:skel] - jnp.where(half, f[n][:skel], f[n][skel : 2 * skel])
            for s in range(slots):
                coup_out[b, s] = coupled[:, 2 * s * skel : 2 * (s + 1) * skel]
                one = u[n][s * skel : (s + 1) * skel, 2 * s * skel : (2 * s + 1) * skel]
                packed = jnp.concatenate([one[: skel // 2], one[skel // 2 :]], 1)
                at = b - offset_of(s) + REACH
                sums[at] = sums[at] + packed

    leaving = jnp.where(first_half, boxes + REACH, 0)
    landing = jnp.where(first_half, REACH, boxes)
    u_copy = pltpu.make_async_remote_copy(
        src_ref=sums.at[pl.ds(leaving, REACH)], dst_ref=arrived, send_sem=u_sem.at[0],
        recv_sem=u_sem.at[1], device_id=(near_device, q), device_id_type=MESH)
    spans = [jnp.abs(offset_of(s)) for s in range(slots)]
    longest = functools.reduce(jnp.maximum, spans)
    shortest = functools.reduce(jnp.minimum, spans)
    peers = (across, corner, pair)

    def ready_at(c):
        seen = jnp.where(first_half, c, boxes - 1 - c)
        last = boxes - 1 - jnp.maximum(seen - longest, 0)
        last = jnp.where(seen >= shortest, last, 0)
        return jnp.where(seen < REACH, jnp.maximum(last, boxes - 3), last) // 2

    def sum_copy(k, c):
        return pltpu.make_async_remote_copy(
            src_ref=sums.at[c + REACH], dst_ref=others.at[k, c], send_sem=n_send.at[k, c],
            recv_sem=n_recv.at[k, c], device_id=(place, peers[k]), device_id_type=MESH)

    def main(trip, carry):
        bs = [box_at(2 * trip), box_at(2 * trip + 1)]
        factor(bs)

        @pl.when(trip == 0)
        def _():
            mask_copy.wait()

        @pl.when(trip + 1 < boxes // 2)
        def _():
            forward(box_at(2 * trip + 2))
            forward(box_at(2 * trip + 3))

        slot_step(bs)

        @pl.when(trip == REACH // 2 - 1)
        def _():
            u_copy.start()

        @pl.when(trip == (boxes - 3) // 2)
        def _():
            u_copy.wait()
            sums[pl.ds(landing, REACH)] = sums[pl.ds(landing, REACH)] + arrived[...]

        def share(c, carry):
            @pl.when(ready_at(c) == trip)
            def _():
                for k in range(len(peers)):
                    sum_copy(k, c).start()
            return carry

        lax.fori_loop(0, boxes, share, 0)
        return carry

    early = 3
    lax.fori_loop(0, early, prepare, 0)
    pl.semaphore_wait(barrier, 5)
    lax.fori_loop(0, boxes, start, 0)
    mask_copy.start()
    lax.fori_loop(0, boxes, start_far, 0)
    lax.fori_loop(early, boxes, prepare, 0)
    forward(box_at(0))
    forward(box_at(1))
    lax.fori_loop(0, boxes // 2, main, 0)
    lax.fori_loop(0, boxes, done_sends, 0)

    def band_done(step, carry):
        b = box_at(step)
        for s in range(slots):
            @pl.when(is_far(b, s))
            def _():
                band_far(b, s, source_of(b, s)).wait_send()
        return carry

    lax.fori_loop(0, boxes, band_done, 0)

    def finish(c, carry):
        for k in range(len(peers)):
            sum_copy(k, c).wait()
        total = (sums[c + REACH] + others[0, c]) + (others[1, c] + others[2, c])
        full = jnp.concatenate([total[:, :skel], total[:, skel:]], 0)
        skel_out[c] = own[c] - full
        return carry

    lax.fori_loop(0, boxes, finish, 0)


def deliver_kernel(count, *refs):
    sems = refs[-1]
    copies = [
        pltpu.make_async_copy(refs[n], refs[count + n], sems.at[n]) for n in range(count)]
    for copy in copies:
        copy.start()
    for copy in copies:
        copy.wait()


def deliver(arrays):
    anywhere = pl.BlockSpec(memory_space=pl.ANY)
    return pl.pallas_call(
        functools.partial(deliver_kernel, len(arrays)),
        out_shape=tuple(jax.ShapeDtypeStruct(a.shape, a.dtype) for a in arrays),
        in_specs=[anywhere] * len(arrays),
        out_specs=[anywhere] * len(arrays),
        scratch_shapes=[pltpu.SemaphoreType.DMA((len(arrays),))],
        compiler_params=pltpu.CompilerParams(vmem_limit_bytes=1024 * 1024),
        name="deliver",
    )(*arrays)


def body(box_devs, nbr_devs, self_block, ordering, interp, near_band, pair_mask):
    boxes, rows, pts = self_block.shape
    skel, red = interp.shape[1:]
    slots = near_band.shape[1]
    f32, bf16 = jnp.float32, jnp.bfloat16
    vmem = pl.BlockSpec(memory_space=pltpu.VMEM)
    hbm = pl.BlockSpec(memory_space=pltpu.HBM)
    dma = pltpu.SemaphoreType.DMA
    results = pl.pallas_call(
        functools.partial(kernel, box_devs, nbr_devs, skel),
        out_shape=(
            jax.ShapeDtypeStruct((boxes, skel, skel), f32),
            jax.ShapeDtypeStruct((boxes, red // nbr_devs, red), f32),
            jax.ShapeDtypeStruct((boxes, slots, skel, 2 * skel), f32),
        ),
        in_specs=[hbm, vmem, vmem, hbm, vmem],
        out_specs=(vmem, vmem, vmem),
        scratch_shapes=[
            pltpu.VMEM((boxes, pts, pts), f32),
            pltpu.VMEM((boxes, slots, 2, skel, pts), f32),
            pltpu.VMEM(pair_mask.shape[::-1], jnp.int32),
            pltpu.VMEM((2, red, red), f32),
            pltpu.VMEM((boxes, pts, pts), bf16),
            pltpu.VMEM((boxes, red, pts), bf16),
            pltpu.VMEM((boxes, 2 * skel + red, red), bf16),
            pltpu.VMEM((boxes, 2 * skel + red, red), bf16),
            pltpu.VMEM((boxes, skel, skel), f32),
            pltpu.VMEM((boxes + 2 * REACH, skel // 2, 2 * skel), f32),
            pltpu.VMEM((REACH, skel // 2, 2 * skel), f32),
            pltpu.VMEM((nbr_devs - 1, boxes, skel // 2, 2 * skel), f32),
            dma((boxes,)),
            dma((3, boxes)),
            dma((3, boxes)),
            dma((boxes, slots)),
            dma((boxes, slots)),
            dma((2,)),
            dma((2,)),
            dma((nbr_devs - 1, boxes)),
            dma((nbr_devs - 1, boxes)),
        ],
        compiler_params=pltpu.CompilerParams(
            collective_id=0, has_side_effects=True, vmem_limit_bytes=52 * 1024 * 1024),
        name="level",
    )(*[
        pltpu.with_memory_space_constraint(a, pltpu.HBM)
        for a in (self_block, ordering, interp, near_band, pair_mask.T)])
    return deliver(results)


def solution(mesh):
    placed = (
        P("box", "nbr", None),
        P("box", None),
        P("box", None, None),
        P("box", "nbr", None, None, None),
        P("box", "nbr"),
    )
    return jax.shard_map(
        functools.partial(body, mesh.shape["box"], mesh.shape["nbr"]),
        mesh=mesh,
        in_specs=placed,
        out_specs=(P("box", None, None), P("box", "nbr", None), P("box", "nbr", None, None)),
        check_vma=False,
    )
```
